128 devices in a mesh: slab: 16 (over z, x), orb: 8 (over y, core).
Axes of the slice: x: 4, y: 4, z: 4, core: 2. Of those that a mesh axis runs over, the one named last changes fastest.
Arguments:
- orbitals: bfloat16 [4096, 128, 256], P(('slab', 'orb')), may hold values from -12 to 12
- region_start: int32 [4096], P(('slab', 'orb')), may hold values from 0 to 2047, as said below
- kin_cross: bfloat16 [256, 256], replicated, may hold values from -0.375 to 0.375
- potential: float32 [2048, 256], P(('slab', 'orb')), may hold values from 0.5 to 2
- pattern: int32 [64, 5], replicated, may hold values from 0 to 63, as said below
Outputs:
- gradient: bfloat16 [4096, 128, 256], P(('slab', 'orb'))
The draws below stay inside these ranges and needn't reach their ends.
Inputs may be any that keep to these rules, and one draw needn't show every extreme that they name: `region_start`: region_start_i - (i // 256) * 128 lies in 0 to 127 and takes both ends within every slab's orbitals; regions continue periodically past the last grid column. `pattern`: row b lists 5 distinct blocks, b among them, all whose orbitals begin in slab b // 4 or the slab before or after it, taken periodically.
All inputs are finite; a program needn't handle non-finite values.
Results may differ from the reference program's by a relative error of at most 0.0085.
Values may be sent and summed in bfloat16 or wider, within the bound.
No kernel may reach another device: no remote copies, remote signals or barrier semaphores. Data moves between devices by JAX's collectives and lax.ppermute only.
A program may use at most 128 MiB of HBM per device.

```python
import math
import jax
import jax.numpy as jnp
from jax import lax

C = 256
LW = 128
BLOCK = 64
BLK_SLAB = 4
NNB = 5
ORB_SLAB = 256
NORB = 4096
NBLK = 64
NG = 2048
N_SLAB = 16


def region_offsets(key):
    raw = jax.random.randint(jax.random.fold_in(key, 11), (NORB,), 0, LW, dtype=jnp.int32)
    inside = jnp.arange(NORB, dtype=jnp.int32) % ORB_SLAB
    raw = jnp.where(inside == 0, 0, jnp.where(inside == ORB_SLAB - 1, LW - 1, raw))
    return jnp.arange(NORB, dtype=jnp.int32) // ORB_SLAB * LW + raw


def draw_region_start(key, part):
    return region_offsets(key).astype(jnp.int32)


def draw_orbitals(key, part):
    starts = region_offsets(key)
    columns = (starts[:, None] + jnp.arange(LW, dtype=jnp.int32)[None, :]) % NG
    fields = jax.random.normal(jax.random.fold_in(key, 12), (4, NG, C), jnp.float32)
    weights = 0.5 * jax.random.normal(jax.random.fold_in(key, 13), (NORB, 4), jnp.float32)
    noise = jax.random.normal(jax.random.fold_in(key, 14), (NORB, LW, C), jnp.float32)
    total = noise
    for which in range(4):
        total = total + weights[:, which][:, None, None] * fields[which][columns]
    return jnp.clip(total, -12.0, 12.0).astype(jnp.bfloat16)


def draw_pattern(key, part):
    others = 3 * BLK_SLAB - 1
    keys = jax.random.split(jax.random.fold_in(key, 21), NBLK)
    perms = jax.vmap(lambda single: jax.random.permutation(single, others))(keys).astype(jnp.int32)
    blocks = jnp.arange(NBLK, dtype=jnp.int32)
    self_local = BLK_SLAB + blocks % BLK_SLAB
    mapped = jnp.where(perms >= self_local[:, None], perms + 1, perms)
    chosen = jnp.concatenate([self_local[:, None], mapped[:, :NNB - 1]], axis=1)
    slab_of = blocks // BLK_SLAB
    return (((slab_of[:, None] - 1) * BLK_SLAB + chosen) % NBLK).astype(jnp.int32)


def block_scale(own_key, dims, cuts, smallest, top_value):
    gain, own = 1.0, jax.random.fold_in(own_key, 6)
    for axis_at, blocks in cuts:
        steps = jnp.exp(jax.random.uniform(jax.random.fold_in(own, axis_at), (blocks,), jnp.float32, smallest / len(cuts), top_value / len(cuts)))
        gain = gain * jnp.repeat(steps, dims[axis_at] // blocks).reshape([-1 if axis == axis_at else 1 for axis in range(len(dims))])
    return gain


def normal_values(stream_key, shape, spread, most, held_as=jnp.bfloat16):
    drawn = jax.random.normal(stream_key, shape, jnp.float32) * spread
    return jnp.minimum(jnp.maximum(drawn, -most), most).astype(held_as)


def setup_inputs(seed: int = 0) -> dict:
    splits = jax.random.split(jax.random.key(seed), 6)
    return {
        "orbitals": draw_orbitals(jax.random.fold_in(splits[5], 71), 0),
        "region_start": draw_region_start(jax.random.fold_in(splits[5], 71), 0),
        "kin_cross": normal_values(splits[2], (C, C), C ** -0.5, 0.375),
        "potential": jnp.clip(jnp.exp(math.log(2.0) - 1.3862944 * jax.random.uniform(splits[3], (NG, C), jnp.float32) ** block_scale(splits[3], (NG, C), ((0, 128),), -0.2, 0.2)), 0.5, 2.0),
        "pattern": draw_pattern(jax.random.fold_in(splits[5], 71), 0),
    }


def kinetic_term(values, left_col, right_col, kin_cross):
    widen = values.astype(jnp.float32)
    before = jnp.concatenate([left_col, widen[:, :-1]], axis=1)
    after = jnp.concatenate([widen[:, 1:], right_col], axis=1)
    across = jnp.dot(values.reshape(-1, values.shape[2]), kin_cross, preferred_element_type=jnp.float32)
    across = across.reshape(widen.shape)
    return (0.5 * (2.0 * widen - before - after) + across).astype(jnp.bfloat16)


def place_rows(values, offset):
    length = values.shape[1]
    zero_block = jnp.zeros_like(values)
    padded = jnp.concatenate([zero_block, values, zero_block], axis=1)

    def single(orb_row, begin_at):
        return lax.dynamic_slice_in_dim(orb_row, (length - begin_at).astype(jnp.int32), 2 * length, 0)

    return jax.vmap(single)(padded, offset)


def window_rows(values, offset, length):
    def single(orb_row, begin_at):
        return lax.dynamic_slice_in_dim(orb_row, begin_at.astype(jnp.int32), length, 0)

    return jax.vmap(single)(values, offset)


def reference(orbitals, region_start, kin_cross, potential, pattern):
    norb = orbitals.shape[0]
    owner = jnp.arange(norb, dtype=jnp.int32) // ORB_SLAB
    offset = (region_start - owner * LW).astype(jnp.int32)
    edge = jnp.zeros((norb, 1, C), jnp.float32)
    kinetic = kinetic_term(orbitals, edge, edge, kin_cross)
    phi_buf = place_rows(orbitals, offset).reshape(N_SLAB, ORB_SLAB, 2, LW, C)
    kin_buf = place_rows(kinetic, offset).reshape(N_SLAB, ORB_SLAB, 2, LW, C)
    cover = jnp.any(pattern[:, :, None] == jnp.arange(NBLK, dtype=jnp.int32)[None, None, :], axis=1)
    slab_pot = potential.reshape(N_SLAB, LW, C)
    volume = 1.0 / (LW * C)
    scale = 1.0 / (NNB * BLOCK)
    contract_rows = (((1,), (1,)), ((), ()))
    contract_cols = (((0,), (0,)), ((), ()))
    half_count = ORB_SLAB

    def slab_fields(slab_index):
        before = (slab_index - 1) % N_SLAB
        phi_grid = jnp.concatenate([phi_buf[before][:, 1], phi_buf[slab_index][:, 0]], axis=0)
        kin_grid = jnp.concatenate([kin_buf[before][:, 1], kin_buf[slab_index][:, 0]], axis=0)
        applied = (kin_grid.astype(jnp.float32) + slab_pot[slab_index][None] * phi_grid.astype(jnp.float32)).astype(jnp.bfloat16)
        return phi_grid.reshape(2 * ORB_SLAB, LW * C), applied.reshape(2 * ORB_SLAB, LW * C)

    def partial_pairs(slab_index):
        flat_phi, flat_app = slab_fields(slab_index)
        intersection = lax.dot_general(flat_phi, flat_phi, contract_rows, preferred_element_type=jnp.float32) * volume
        hamilton = lax.dot_general(flat_phi, flat_app, contract_rows, preferred_element_type=jnp.float32) * volume
        return intersection, hamilton

    slab_ids = jnp.arange(N_SLAB, dtype=jnp.int32)
    part_over, part_ham = lax.map(partial_pairs, slab_ids)

    def complete(sums):
        prev_bb = jnp.roll(sums[:, half_count:, half_count:], 1, axis=0)
        next_aa = jnp.roll(sums[:, :half_count, :half_count], -1, axis=0)
        sums = sums.at[:, :half_count, :half_count].add(prev_bb)
        return sums.at[:, half_count:, half_count:].add(next_aa)

    full_over = complete(part_over)
    full_ham = complete(part_ham)

    def gradient_slab(slab_index):
        flat_phi, flat_app = slab_fields(slab_index)
        block_ids = ((slab_index - 1) * BLK_SLAB + jnp.arange(2 * BLK_SLAB, dtype=jnp.int32)) % NBLK
        sub_cover = jnp.take(jnp.take(cover, block_ids, axis=0), block_ids, axis=1).astype(jnp.float32)
        orb_cover = jnp.repeat(jnp.repeat(sub_cover, BLOCK, axis=0), BLOCK, axis=1)
        masked_intersection = (full_over[slab_index] * orb_cover).astype(jnp.bfloat16)
        masked_hamilton = (full_ham[slab_index] * orb_cover).astype(jnp.bfloat16)
        first = lax.dot_general(masked_intersection, flat_app, contract_cols, preferred_element_type=jnp.float32)
        second = lax.dot_general(masked_hamilton, flat_phi, contract_cols, preferred_element_type=jnp.float32)
        return ((first - second) * scale).astype(jnp.bfloat16).reshape(2 * ORB_SLAB, LW, C)

    grads = lax.map(gradient_slab, slab_ids)
    own_part = grads[:, half_count:]
    next_part = jnp.roll(grads[:, :half_count], -1, axis=0)
    buffers = jnp.concatenate([own_part, next_part], axis=2).reshape(norb, 2 * LW, C)
    return window_rows(buffers, offset, LW)
```

```python
import functools
import jax
import jax.numpy as jnp
from jax import lax
from jax.experimental import pallas as pl
from jax.experimental.pallas import tpu as pltpu
from jax.sharding import PartitionSpec as P

BLOCK = 64
CHUNKS = 2
F32 = jnp.float32
BF16 = jnp.bfloat16
NT = (((1,), (1,)), ((), ()))
NN = (((1,), (0,)), ((), ()))


def params():
    return pltpu.CompilerParams(vmem_limit_bytes=56 * 1024 * 1024)


def vmem():
    return pl.BlockSpec(memory_space=pltpu.VMEM)


def smem():
    return pl.BlockSpec(memory_space=pltpu.SMEM)


def spread_kernel(start_ref, where_ref, x_ref, *rest, chunks, peers):
    outs, scratch = rest[:chunks], rest[chunks]
    held, length, cross = x_ref.shape
    each = held // chunks
    narrow = length // peers
    base = where_ref[0] * length + length // 2
    gap = (
        lax.broadcasted_iota(jnp.int32, (length, length), 0)
        - lax.broadcasted_iota(jnp.int32, (length, length), 1)
    ) & (length - 1)
    for which in range(chunks):
        for j in range(each):
            orb = which * each + j
            shift = (start_ref[orb] - base) & (length - 1)
            pick = jnp.where(gap == shift, 1.0, 0.0).astype(BF16)
            rolled = jnp.dot(pick, x_ref[orb], preferred_element_type=F32)
            for lane in range(0, cross, 128):
                scratch[lane // 128, pl.ds(j, length, stride=each), :] = rolled[:, lane : lane + 128]
        for peer in range(peers):
            group = (peer % 2) * (peers // 2) + peer // 2
            for q in range(narrow + 2):
                row = (group * narrow - 1 + q) % length
                for half in range(cross // 128):
                    outs[which][peer, q, :, half * 128 : half * 128 + 128] = scratch[
                        half, row * each : (row + 1) * each, :
                    ].astype(BF16)


def collect_kernel(start_ref, where_ref, *rest, chunks, peers):
    ins, out_ref, scratch = rest[:chunks], rest[chunks], rest[chunks + 1]
    held, length, cross = out_ref.shape
    each = held // chunks
    narrow = length // peers
    base = where_ref[0] * length + length // 2
    gap = (
        lax.broadcasted_iota(jnp.int32, (length, length), 1)
        - lax.broadcasted_iota(jnp.int32, (length, length), 0)
    ) & (length - 1)
    for which in range(chunks):
        for peer in range(peers):
            group = (peer % 2) * (peers // 2) + peer // 2
            for q in range(narrow):
                row = group * narrow + q
                for half in range(cross // 128):
                    scratch[half, row * each : (row + 1) * each, :] = ins[which][
                        peer, q, :, half * 128 : half * 128 + 128
                    ].astype(F32)
        for j in range(each):
            orb = which * each + j
            shift = (start_ref[orb] - base) & (length - 1)
            pick = jnp.where(gap == shift, 1.0, 0.0).astype(BF16)
            rows = jnp.concatenate(
                [scratch[half, pl.ds(j, length, stride=each), :] for half in range(cross // 128)], axis=1
            ).astype(BF16)
            out_ref[orb] = jnp.dot(pick, rows, preferred_element_type=F32).astype(BF16)


def make_fields(pieces, offset, position, own, pot_ref, kin_cross, phi_ref, app_ref, quad):
    cross = kin_cross.shape[0]

    def at(q):
        tile = jnp.concatenate([piece[:, q] for piece in pieces], axis=1)
        return tile.reshape(-1, cross)

    phis, apps = [], []
    for step in range(4):
        col = quad * 4 + step
        place = position + col - offset
        inside = (place >= 0) & (place < 128)
        if not own:
            inside = jnp.logical_not(inside)
        row = place & 127
        keep = jnp.where(inside, 1.0, 0.0)
        left = jnp.where(row == 0, 0.0, keep)
        right = jnp.where(row == 127, 0.0, keep)
        phi = at(col + 1).astype(F32) * keep
        phi_low = phi.astype(BF16)
        across = jnp.dot(phi_low, kin_cross, preferred_element_type=F32)
        before = at(col).astype(F32) * left
        after = at(col + 2).astype(F32) * right
        kin = (0.5 * (2.0 * phi - before - after) + across).astype(BF16).astype(F32)
        apps.append((kin + pot_ref[col : col + 1, :] * phi).astype(BF16))
        phis.append(phi_low)
    phi = jnp.concatenate(phis, axis=1)
    app = jnp.concatenate(apps, axis=1)
    phi_ref[quad] = phi
    app_ref[quad] = app
    return phi, app


def own_kernel(place_ref, off_ref, pot_ref, kin_ref, *rest, chunks):
    pieces, (phi_ref, app_ref, pair_ref) = rest[:chunks], rest[chunks:]
    quads, count, _ = phi_ref.shape
    offset = off_ref[...]
    kin_cross = kin_ref[...]
    for quad in range(quads):
        phi, app = make_fields(
            pieces, offset, place_ref[0], True, pot_ref, kin_cross, phi_ref, app_ref, quad
        )
        both = jnp.concatenate([phi, app], axis=0)
        term = lax.dot_general(both, phi, NT, preferred_element_type=F32)
        if quad == 0:
            pair_ref[...] = term
        else:
            pair_ref[...] += term


def local_block(pattern_ref, home, near, block, slot, per_slab, total):
    base = jnp.where(block < per_slab, home, near)
    listed = pattern_ref[base * per_slab + block % per_slab, slot]
    slab = listed // per_slab
    inner = listed % per_slab
    return jnp.where(slab == home, inner, jnp.where(slab == near, per_slab + inner, 2 * per_slab))


def pair_kernel(
    place_ref, pattern_ref, off_ref, pot_ref, kin_ref, pair_ref, phi_own_ref, app_own_ref, *rest,
    chunks, scale
):
    pieces = rest[:chunks]
    phi_ref, app_ref = rest[chunks : chunks + 2]
    outs = rest[chunks + 2 : chunks + 6]
    table = rest[chunks + 6]
    quads, count, _ = phi_ref.shape
    offset = off_ref[...]
    kin_cross = kin_ref[...]
    for quad in range(quads):
        phi, app = make_fields(
            pieces, offset, place_ref[0], False, pot_ref, kin_cross, phi_ref, app_ref, quad
        )
        phi_own = phi_own_ref[quad]
        app_own = app_own_ref[quad]
        every = jnp.concatenate([phi_own, phi, app_own, app], axis=0)
        near = lax.dot_general(every, phi, NT, preferred_element_type=F32)
        both = jnp.concatenate([phi, app], axis=0)
        home = lax.dot_general(both, phi_own, NT, preferred_element_type=F32)
        for kind in range(2):
            rows = near[kind * 2 * count : (kind + 1) * 2 * count]
            part = home[kind * count : (kind + 1) * count]
            if quad == 0:
                table[kind, : 2 * count, count:] = rows
                table[kind, count : 2 * count, :count] = part
            else:
                table[kind, : 2 * count, count:] += rows
                table[kind, count : 2 * count, :count] += part
    for kind in range(2):
        table[kind, :count, :count] = pair_ref[kind * count : (kind + 1) * count]
        table[kind, 2 * count :, :] = jnp.zeros_like(table[kind, 2 * count :, :])
    low = lax.broadcasted_iota(jnp.int32, (16, 128), 1) < BLOCK
    per_slab = count // BLOCK
    for group in range(2 * count // 128):
        for slot in range(5):
            first, second = [
                local_block(
                    pattern_ref, place_ref[1], place_ref[2], 2 * group + side, slot, per_slab, 0
                )
                * BLOCK
                for side in range(2)
            ]
            for step in range(4):
                quarter = ((place_ref[3] + step) & 3) * 16
                for kind in range(2):
                    lanes = slice(group * 128, group * 128 + 128)
                    one = table[kind, pl.ds(pl.multiple_of(first + quarter, 16), 16), lanes]
                    two = table[kind, pl.ds(pl.multiple_of(second + quarter, 16), 16), lanes]
                    outs[step][kind, slot * 16 : slot * 16 + 16, lanes] = (
                        jnp.where(low, one, two) * scale
                    )


def unpack_kernel(place_ref, pattern_ref, *rest):
    homes, nears, out_ref = rest[:4], rest[4:8], rest[8]
    total = out_ref.shape[0]
    count = total // 2
    per_slab = count // BLOCK
    low = lax.broadcasted_iota(jnp.int32, (16, 128), 1) < BLOCK
    for group in range(total // 128):
        refs = homes if group < count // 128 else nears
        lanes = slice((group * 128) % count, (group * 128) % count + 128)
        found = []
        for slot in range(5):
            first, second = [
                local_block(
                    pattern_ref, place_ref[1], place_ref[2], 2 * group + side, slot, per_slab, 0
                )
                for side in range(2)
            ]
            found.append(jnp.where(low, first, second))
        for block in range(2 * per_slab):
            hits = [jnp.where(found[slot] == block, 1.0, 0.0) for slot in range(5)]
            for step in range(4):
                quarter = ((place_ref[3] - step) & 3) * 16
                for kind in range(2):
                    acc = jnp.zeros((16, 128), F32)
                    for slot in range(5):
                        part = refs[step][kind, slot * 16 : slot * 16 + 16, lanes].astype(F32)
                        acc = acc + part * hits[slot]
                    if kind == 1:
                        acc = -acc
                    out_ref[
                        pl.ds(pl.multiple_of(block * BLOCK + quarter, 16), 16),
                        kind * total + group * 128 : kind * total + group * 128 + 128,
                    ] = acc.astype(BF16)


def gradient_kernel(
    place_ref, off_ref, mat_ref, phi_own_ref, app_own_ref, phi_ref, app_ref, *outs, own, scale
):
    quads, count, wide = phi_ref.shape
    cross = wide // 4
    chunks = len(outs)
    peers, _, each, _ = outs[0].shape
    offset = off_ref[...]
    first = 0 if own else count
    mat = mat_ref[first : first + count]
    for quad in range(quads):
        right = jnp.concatenate(
            [app_own_ref[quad], app_ref[quad], phi_own_ref[quad], phi_ref[quad]], axis=0
        )
        grad = jnp.dot(mat, right, preferred_element_type=F32) * scale
        for step in range(4):
            col = quad * 4 + step
            place = place_ref[0] + col - offset
            inside = (place >= 0) & (place < 128)
            if not own:
                inside = jnp.logical_not(inside)
            part = jnp.where(inside, grad[:, step * cross : (step + 1) * cross], 0.0).astype(BF16)
            part = part.reshape(peers, chunks * each, cross)
            for which in range(chunks):
                outs[which][:, col] = part[:, which * each : (which + 1) * each]


def per_device(orbitals, region_start, kin_cross, potential, pattern):
    held, length, cross = orbitals.shape
    peers = lax.axis_size("orb")
    slabs = lax.axis_size("slab")
    slab_id = lax.axis_index("slab").astype(jnp.int32)
    orb_id = lax.axis_index("orb").astype(jnp.int32)
    core, level = orb_id % 2, orb_id // 2
    levels = peers // 2
    count = held * peers
    narrow = length // peers
    each = held // CHUNKS
    quads = narrow // 4
    axes = ("slab", "orb")

    def send(array, route):
        pairs = []
        for s in range(slabs):
            for k in range(peers):
                ds, dk = route(k % 2, k // 2)
                if ds is None:
                    continue
                pairs.append((s * peers + k, ((s + ds) % slabs) * peers + dk))
        return lax.ppermute(array, axes, pairs)

    def onward(array):
        return send(array, lambda c, y: ((1, 2 * y) if c == 0 else (-1, 2 * y + 1)))

    def back(array):
        return send(array, lambda c, y: ((-1, 2 * y) if c == 0 else (1, 2 * y + 1)))

    def around(array, by):
        return send(array, lambda c, y: (0, 2 * ((y + by) % levels) + c))

    near_id = jnp.where(core == 0, slab_id - 1, slab_id + 1) % slabs
    position = (core * levels + level) * narrow + length // 2
    place = jnp.stack([position, slab_id, near_id, level])

    pot_pairs = []
    for s in range(slabs):
        for k in range(peers):
            if k >= levels:
                pot_pairs.append((s * peers + k, s * peers + 2 * (k - levels)))
            else:
                pot_pairs.append((s * peers + k, ((s - 1) % slabs) * peers + 2 * k + 1))
    window_pot = lax.ppermute(potential, axes, pot_pairs)
    starts = lax.all_to_all(
        jnp.broadcast_to(region_start[None], (peers, held)), "orb", 0, 0, tiled=True
    ).reshape(count, 1)
    off_own = starts - slab_id * length
    off_near = onward(off_own)

    scratch = pltpu.VMEM((cross // 128, length * each, 128), F32)
    pieces = pl.pallas_call(
        functools.partial(spread_kernel, chunks=CHUNKS, peers=peers),
        out_shape=[jax.ShapeDtypeStruct((peers, narrow + 2, each, cross), BF16)] * CHUNKS,
        in_specs=[smem(), smem(), vmem()],
        out_specs=[vmem()] * CHUNKS,
        scratch_shapes=[scratch],
        compiler_params=params(),
        name="spread",
    )(region_start, slab_id.reshape(1), orbitals)
    mine = [lax.all_to_all(piece, "orb", 0, 0, tiled=True) for piece in pieces]
    moved = [onward(piece) for piece in mine]

    field = jax.ShapeDtypeStruct((quads, count, 4 * cross), BF16)
    phi_own, app_own, pair = pl.pallas_call(
        functools.partial(own_kernel, chunks=CHUNKS),
        out_shape=[field, field, jax.ShapeDtypeStruct((2 * count, count), F32)],
        in_specs=[smem()] + [vmem()] * (3 + CHUNKS),
        out_specs=[vmem()] * 3,
        compiler_params=params(),
        name="own",
    )(place, off_own, window_pot, kin_cross, *mine)
    packed = jax.ShapeDtypeStruct((2, 5 * 16, 2 * count), F32)
    phi_near, app_near, *parts = pl.pallas_call(
        functools.partial(pair_kernel, chunks=CHUNKS, scale=1.0 / (length * cross)),
        out_shape=[field, field] + [packed] * 4,
        in_specs=[smem(), smem()] + [vmem()] * (6 + CHUNKS),
        out_specs=[vmem()] * 6,
        scratch_shapes=[pltpu.VMEM((2, 2 * count + BLOCK, 2 * count), F32)],
        compiler_params=params(),
        name="pair",
    )(place, pattern, off_near, window_pot, kin_cross, pair, phi_own, app_own, *moved)

    total = parts[0]
    for by in range(1, levels):
        total = total + around(parts[by], by)
    home, near = total[:, :, :count], total[:, :, count:]
    other = send(home, lambda c, y: (0, 2 * y + 1 - c))
    same = back(near)
    cross_over = send(near, lambda c, y: ((-1, 2 * y + 1) if c == 0 else (1, 2 * y)))
    done = (home + other + same + cross_over).astype(BF16)
    homes = [done] + [around(done, by) for by in range(1, levels)]
    nears = []
    for by in range(levels):
        nears.append(
            send(
                done,
                lambda c, y, by=by: (
                    (1, 2 * ((y + by) % levels)) if c == 0 else (-1, 2 * ((y + by) % levels) + 1)
                ),
            )
        )
    mat = pl.pallas_call(
        unpack_kernel,
        out_shape=jax.ShapeDtypeStruct((2 * count, 4 * count), BF16),
        in_specs=[smem(), smem()] + [vmem()] * 8,
        out_specs=vmem(),
        compiler_params=params(),
        name="unpack",
    )(place, pattern, *homes, *nears)

    def gradient(own, offset):
        return pl.pallas_call(
            functools.partial(gradient_kernel, own=own, scale=1.0 / (pattern.shape[1] * BLOCK)),
            out_shape=[jax.ShapeDtypeStruct((peers, narrow, each, cross), BF16)] * CHUNKS,
            in_specs=[smem()] + [vmem()] * 6,
            out_specs=[vmem()] * CHUNKS,
            compiler_params=params(),
            name="gradient",
        )(place, offset, mat, phi_own, app_own, phi_near, app_near)

    grad_near = gradient(False, off_near)
    returned = [back(item) for item in grad_near]
    grad_own = gradient(True, off_own)
    joined = [a + b for a, b in zip(grad_own, returned)]
    owned = [lax.all_to_all(item, "orb", 0, 0, tiled=True) for item in joined]
    return pl.pallas_call(
        functools.partial(collect_kernel, chunks=CHUNKS, peers=peers),
        out_shape=jax.ShapeDtypeStruct(orbitals.shape, BF16),
        in_specs=[smem(), smem()] + [vmem()] * CHUNKS,
        out_specs=vmem(),
        scratch_shapes=[scratch],
        compiler_params=params(),
        name="collect",
    )(region_start, slab_id.reshape(1), *owned)


def solution(mesh):
    placed = (
        P(("slab", "orb"), None, None),
        P(("slab", "orb")),
        P(),
        P(("slab", "orb"), None),
        P(),
    )
    return jax.shard_map(
        per_device,
        mesh=mesh,
        in_specs=placed,
        out_specs=P(("slab", "orb"), None, None),
        check_vma=False,
    )
```

```python
import functools
import jax
import jax.numpy as jnp
from jax import lax
from jax.experimental import pallas as pl
from jax.experimental.pallas import tpu as pltpu
from jax.sharding import PartitionSpec as P

BLOCK = 64
CUTS = (0, 2, 4)
F32 = jnp.float32
BF16 = jnp.bfloat16
PARTIAL = BF16
NT = (((1,), (1,)), ((), ()))


def params():
    return pltpu.CompilerParams(vmem_limit_bytes=56 * 1024 * 1024)


def smem():
    return pl.BlockSpec(memory_space=pltpu.SMEM)


def fixed(*shape):
    return pl.BlockSpec(shape, lambda t: (0,) * len(shape))


def shaped(shape, dtype=BF16):
    return jax.ShapeDtypeStruct(shape, dtype)


def other_core(place_ref, side):
    return place_ref[4] if side == 0 else 1 - place_ref[4]


def spread_kernel(start_ref, place_ref, x_ref, *rest, cuts):
    outs, scratch = rest[:-1], rest[-1]
    held, length, cross = x_ref.shape
    levels = 4
    narrow = length // (2 * levels)
    base = place_ref[1] * length
    gap = (
        lax.broadcasted_iota(jnp.int32, (length, length), 0)
        - lax.broadcasted_iota(jnp.int32, (length, length), 1)
    ) & (length - 1)
    which_row = lax.broadcasted_iota(jnp.int32, (held, cross), 0)
    offsets = jnp.zeros((held, cross), jnp.int32)
    for j in range(held):
        offset = start_ref[pl.program_id(0) * held + j] - base
        offsets = jnp.where(which_row == j, offset, offsets)
        shift = (offset + length // 2) & (length - 1)
        pick = jnp.where(gap == shift, 1.0, 0.0).astype(BF16)
        rolled = jnp.dot(pick, x_ref[j], preferred_element_type=F32)
        for half in range(cross // 128):
            scratch[half, pl.ds(j, length, stride=held), :] = rolled[:, half * 128 : half * 128 + 128]
    offsets = offsets.astype(F32).astype(BF16)
    for d in range(levels):
        for side in range(2):
            group = other_core(place_ref, side) * levels + ((place_ref[3] + d) & (levels - 1))
            outs[d][side, 0] = offsets
            for which, (first, last) in enumerate(spans(cuts)):
                for q in range(first, last):
                    row = (group * narrow + q - 1) & (length - 1)
                    to = q - first + (1 if which == 0 else 0)
                    for half in range(cross // 128):
                        outs[which * levels + d][side, to, :, half * 128 : half * 128 + 128] = scratch[
                            half, pl.ds(pl.multiple_of(row * held, held), held), :
                        ].astype(BF16)


def spans(cuts):
    return [
        (0 if i == 0 else 4 * cuts[i] + 2, 4 * cuts[i + 1] + 2) for i in range(len(cuts) - 1)
    ]


def collect_kernel(start_ref, place_ref, *rest, cuts):
    levels = 4
    out_ref, scratch = rest[-2], rest[-1]
    held, length, cross = out_ref.shape
    narrow = length // (2 * levels)
    base = place_ref[1] * length + length // 2
    gap = (
        lax.broadcasted_iota(jnp.int32, (length, length), 1)
        - lax.broadcasted_iota(jnp.int32, (length, length), 0)
    ) & (length - 1)
    for which in range(len(cuts) - 1):
        wide = 4 * (cuts[which + 1] - cuts[which])
        for d in range(levels):
            for side in range(2):
                group = other_core(place_ref, side) * levels + ((place_ref[3] - d) & (levels - 1))
                first = (group * narrow + 4 * cuts[which]) * held
                for half in range(cross // 128):
                    scratch[half, pl.ds(pl.multiple_of(first, 4 * held), wide * held), :] = (
                        rest[which * levels + d][side, :, :, half * 128 : half * 128 + 128]
                        .reshape(wide * held, 128)
                        .astype(F32)
                    )
    for j in range(held):
        shift = (start_ref[pl.program_id(0) * held + j] - base) & (length - 1)
        pick = jnp.where(gap == shift, 1.0, 0.0).astype(BF16)
        rows = jnp.concatenate(
            [scratch[half, pl.ds(j, length, stride=held), :] for half in range(cross // 128)], axis=1
        ).astype(BF16)
        out_ref[j] = jnp.dot(pick, rows, preferred_element_type=F32).astype(BF16)


def make_fields(place_ref, pot_ref, kin_ref, off_ref, row_at, across_ref, phi_ref, app_ref, *, own, start):
    cross = kin_ref.shape[0]
    quads, count, _ = phi_ref.shape
    levels = 4
    held = count // (2 * levels)
    units = [(d, side) for d in range(levels) for side in range(2)]
    places = [
        pl.multiple_of(
            (((place_ref[3] - d) & (levels - 1)) * 2 + other_core(place_ref, side)) * held, held
        )
        for d, side in units
    ]
    for col in range(4 * quads):
        lanes = slice((col % 4) * cross, (col % 4 + 1) * cross)
        now = start * 4 + col
        for (d, side), at in zip(units, places):
            place = place_ref[0] + now - off_ref[pl.ds(at, held), :].astype(jnp.int32)
            inside = (place >= 0) & (place < 128)
            keep = jnp.where(inside, 1.0, 0.0) if own else jnp.where(inside, 0.0, 1.0)
            keep = jnp.concatenate([keep, keep], axis=1)
            phi_ref[col // 4, pl.ds(at, held), lanes] = (
                row_at(side, d, now + 1).astype(F32) * keep
            ).astype(BF16)
        across_ref[...] = jnp.dot(
            phi_ref[col // 4, :, lanes], kin_ref[...], preferred_element_type=F32
        )
        for (d, side), at in zip(units, places):
            place = place_ref[0] + now - off_ref[pl.ds(at, held), :].astype(jnp.int32)
            inside = (place >= 0) & (place < 128)
            keep = jnp.where(inside, 0.5, 0.0) if own else jnp.where(inside, 0.0, 0.5)
            row = place & 127
            left = jnp.where(row == 0, 0.0, keep)
            right = jnp.where(row == 127, 0.0, keep)
            left = jnp.concatenate([left, left], axis=1)
            right = jnp.concatenate([right, right], axis=1)
            phi = phi_ref[col // 4, pl.ds(at, held), lanes].astype(F32)
            around = row_at(side, d, now).astype(F32) * left + row_at(side, d, now + 2).astype(F32) * right
            kin = (phi - around + across_ref[pl.ds(at, held), :]).astype(BF16).astype(F32)
            app_ref[col // 4, pl.ds(at, held), lanes] = (
                kin + pot_ref[now : now + 1, :] * phi
            ).astype(BF16)


def chunk_inputs(refs, which, cuts):
    if which == 0:
        pair, rest = refs[:2], refs[2:]

        def row_at(side, d, q):
            return pair[side][d, q + 1]

        return row_at, rest
    pair, edges, rest = refs[:2], refs[2:6], refs[6:]
    first = spans(cuts)[which][0]

    def row_at(side, d, q):
        if q >= first:
            return pair[side][d, q - first]
        return edges[2 * side + q - first + 2][d, 0]

    return row_at, rest


def own_kernel(place_ref, pot_ref, kin_ref, *refs, which, cuts):
    row_at, rest = chunk_inputs(refs, which, cuts)
    if which == 0:
        phi_ref, app_ref, pair_ref, off_ref, across_ref = rest
        store_offsets(place_ref, refs, off_ref)
    else:
        off_ref, before_ref, phi_ref, app_ref, pair_ref, across_ref = rest
    make_fields(
        place_ref, pot_ref, kin_ref, off_ref, row_at, across_ref, phi_ref, app_ref,
        own=True, start=cuts[which],
    )
    for quad in range(phi_ref.shape[0]):
        phi = phi_ref[quad]
        both = jnp.concatenate([phi, app_ref[quad]], axis=0)
        term = lax.dot_general(both, phi, NT, preferred_element_type=F32)
        if quad > 0:
            pair_ref[...] += term
        elif which == 0:
            pair_ref[...] = term
        else:
            pair_ref[...] = before_ref[...] + term


def store_offsets(place_ref, refs, off_ref):
    levels, _, held, _ = refs[0].shape
    for side in range(2):
        for d in range(levels):
            unit = ((place_ref[3] - d) & (levels - 1)) * 2 + other_core(place_ref, side)
            off_ref[pl.ds(pl.multiple_of(unit * held, held), held), :] = refs[side][d, 0][:, :128].astype(F32)


def near_kernel(place_ref, pattern_ref, pot_ref, kin_ref, *refs, which, cuts, scale):
    row_at, rest = chunk_inputs(refs, which, cuts)
    last = which == len(cuts) - 2
    phi_own_ref, app_own_ref, rest = rest[0], rest[1], rest[2:]
    if last:
        pair_ref, rest = rest[0], rest[1:]
    if which == 0:
        phi_ref, app_ref, off_ref, rest = rest[0], rest[1], rest[2], rest[3:]
        store_offsets(place_ref, refs, off_ref)
    else:
        off_ref, before_ref, phi_ref, app_ref, rest = rest[0], rest[1], rest[2], rest[3], rest[4:]
    if last:
        outs, table, across_ref = rest[:4], rest[4], rest[5]
    else:
        table, across_ref = rest
    make_fields(
        place_ref, pot_ref, kin_ref, off_ref, row_at, across_ref, phi_ref, app_ref,
        own=False, start=cuts[which],
    )
    count = phi_ref.shape[1]
    for quad in range(phi_ref.shape[0]):
        phi_own, app_own, phi, app = phi_own_ref[quad], app_own_ref[quad], phi_ref[quad], app_ref[quad]
        every = jnp.concatenate([phi_own, phi, app_own, app], axis=0)
        near = lax.dot_general(every, phi, NT, preferred_element_type=F32)
        both = jnp.concatenate([phi, app], axis=0)
        home = lax.dot_general(both, phi_own, NT, preferred_element_type=F32)
        for kind in range(2):
            right = near[kind * 2 * count : (kind + 1) * 2 * count]
            left = home[kind * count : (kind + 1) * count]
            if quad > 0:
                table[kind, : 2 * count, count:] += right
                table[kind, count : 2 * count, :count] += left
            elif which > 0:
                table[kind, : 2 * count, count:] = right + before_ref[kind, : 2 * count, count:]
                table[kind, count : 2 * count, :count] = (
                    left + before_ref[kind, count : 2 * count, :count]
                )
            else:
                table[kind, : 2 * count, count:] = right
                table[kind, count : 2 * count, :count] = left
    if not last:
        return
    for kind in range(2):
        table[kind, :count, :count] = pair_ref[kind * count : (kind + 1) * count]
        table[kind, 2 * count :, :] = jnp.zeros_like(table[kind, 2 * count :, :])
    low = lax.broadcasted_iota(jnp.int32, (16, 128), 1) < BLOCK
    per_slab = count // BLOCK
    for group in range(2 * count // 128):
        for slot in range(5):
            first, second = [
                local_block(place_ref, pattern_ref, 2 * group + side, slot, per_slab) * BLOCK
                for side in range(2)
            ]
            for by in range(4):
                quarter = ((place_ref[3] + by) & 3) * 16
                for kind in range(2):
                    lanes = slice(group * 128, group * 128 + 128)
                    one = table[kind, pl.ds(pl.multiple_of(first + quarter, 16), 16), lanes]
                    two = table[kind, pl.ds(pl.multiple_of(second + quarter, 16), 16), lanes]
                    outs[by][kind, slot * 16 : slot * 16 + 16, lanes] = (
                        jnp.where(low, one, two) * scale
                    ).astype(outs[by].dtype)


def local_block(place_ref, pattern_ref, block, slot, per_slab):
    home, near = place_ref[1], place_ref[2]
    base = home if block < per_slab else near
    listed = pattern_ref[base * per_slab + block % per_slab, slot]
    slab = listed // per_slab
    inner = listed % per_slab
    return jnp.where(slab == home, inner, jnp.where(slab == near, per_slab + inner, 2 * per_slab))


def unpack_kernel(place_ref, pattern_ref, home_ref, near_ref, out_ref):
    total = out_ref.shape[0]
    per_slab = total // 2 // BLOCK
    low = lax.broadcasted_iota(jnp.int32, (16, 128), 1) < BLOCK
    for group in range(total // 128):
        parts = home_ref if group < total // 256 else near_ref
        first = group * 128 % (total // 2)
        lanes = slice(first, first + 128)
        found = []
        for slot in range(5):
            first, second = [
                local_block(place_ref, pattern_ref, 2 * group + side, slot, per_slab)
                for side in range(2)
            ]
            found.append(jnp.where(low, first, second))
        for block in range(2 * per_slab):
            hits = [jnp.where(found[slot] == block, 1.0, 0.0) for slot in range(5)]
            for by in range(4):
                quarter = (place_ref[3] - by) & 3
                side = (quarter // 2) ^ place_ref[4]
                d = (block % per_slab - place_ref[3]) & 3
                row = ((block // per_slab * 2 + side) * 4 + d) * 32 + (quarter % 2) * 16
                for kind in range(2):
                    acc = jnp.zeros((16, 128), F32)
                    for slot in range(5):
                        part = parts[by, kind, slot * 16 : slot * 16 + 16, lanes].astype(F32)
                        acc = acc + part * hits[slot]
                    if kind == 1:
                        acc = -acc
                    out_ref[
                        pl.ds(pl.multiple_of(row, 16), 16),
                        kind * total + group * 128 : kind * total + group * 128 + 128,
                    ] = acc.astype(BF16)


def gradient_kernel(place_ref, off_own_ref, off_near_ref, mat_ref, *rest, start, scale):
    ins, outs = rest[:4], rest[4:]
    levels, _, held, cross = outs[0].shape
    phi_own_ref, app_own_ref, phi_ref, app_ref = ins
    seats = []
    for ref in (off_own_ref, off_near_ref):
        for side in range(2):
            for d in range(levels):
                unit = ((place_ref[3] + d) & (levels - 1)) * 2 + other_core(place_ref, side)
                seats.append(
                    ref[pl.ds(pl.multiple_of(unit * held, held), held), :].astype(jnp.int32)
                )
    right = jnp.concatenate([app_own_ref[0], app_ref[0], phi_own_ref[0], phi_ref[0]], axis=0)
    grad = jnp.dot(mat_ref[...], right, preferred_element_type=F32)
    base = place_ref[0] + start * 4 + pl.program_id(0) * 4
    for step in range(4):
        for i, seat in enumerate(seats):
            place = base + step - seat
            inside = (place >= 0) & (place < 128)
            own = i < 2 * levels
            keep = jnp.where(inside, scale, 0.0) if own else jnp.where(inside, 0.0, scale)
            keep = jnp.concatenate([keep, keep], axis=1)
            part = grad[i * held : (i + 1) * held, step * cross : (step + 1) * cross] * keep
            outs[i // levels][i % levels, step] = part.astype(BF16)


def body(orbitals, region_start, kin_cross, potential, pattern):
    held, length, cross = orbitals.shape
    peers = lax.axis_size("orb")
    slabs = lax.axis_size("slab")
    slab_id = lax.axis_index("slab").astype(jnp.int32)
    orb_id = lax.axis_index("orb").astype(jnp.int32)
    core, level = orb_id % 2, orb_id // 2
    levels = peers // 2
    count = held * peers
    narrow = length // peers
    axes = ("slab", "orb")
    cuts = CUTS
    chunks = len(cuts) - 1

    def send(array, route):
        pairs = []
        for s in range(slabs):
            for k in range(peers):
                ds, dk = route(k % 2, k // 2)
                pairs.append((s * peers + k, ((s + ds) % slabs) * peers + dk))
        return lax.ppermute(array, axes, pairs)

    def onward(array):
        return send(array, lambda c, y: ((1, 2 * y) if c == 0 else (-1, 2 * y + 1)))

    def back(array):
        return send(array, lambda c, y: ((-1, 2 * y) if c == 0 else (1, 2 * y + 1)))

    def across_up(array):
        return send(array, lambda c, y: ((-1, 2 * y + 1) if c == 0 else (1, 2 * y)))

    def swapped(array):
        return send(array, lambda c, y: (0, 2 * y + 1 - c))

    def around(array, by):
        return send(array, lambda c, y: (0, 2 * ((y + by) % levels) + c))

    near_id = jnp.where(core == 0, slab_id - 1, slab_id + 1) % slabs
    position = (core * levels + level) * narrow + length // 2
    place = jnp.stack([position, slab_id, near_id, level, core])

    pot_pairs = []
    for s in range(slabs):
        for k in range(peers):
            if k >= levels:
                pot_pairs.append((s * peers + k, s * peers + 2 * (k - levels)))
            else:
                pot_pairs.append((s * peers + k, ((s - 1) % slabs) * peers + 2 * k + 1))
    window_pot = lax.ppermute(potential, axes, pot_pairs)

    def call(kernel, outs, ins, args, scratch=(), smems=0, **extra):
        return pl.pallas_call(
            kernel,
            grid=(1,),
            out_shape=outs,
            in_specs=[smem()] * smems + ins,
            out_specs=jax.tree.map(lambda item: fixed(*item.shape), outs),
            scratch_shapes=list(scratch),
            compiler_params=params(),
            **extra,
        )(*args)

    def whole(arrays):
        return [fixed(*item.shape) for item in arrays]

    part = held // 2
    scratch = pltpu.VMEM((cross // 128, length * part, 128), F32)
    deep = [last - first + (1 if i == 0 else 0) for i, (first, last) in enumerate(spans(cuts))]
    by_part = pl.BlockSpec((part, length, cross), lambda t: (t, 0, 0))
    pieces = pl.pallas_call(
        functools.partial(spread_kernel, cuts=cuts),
        grid=(2,),
        out_shape=[shaped((2, rows, held, cross)) for rows in deep for _ in range(levels)],
        in_specs=[smem(), smem(), by_part],
        out_specs=[
            pl.BlockSpec((2, rows, part, cross), lambda t: (0, 0, t, 0))
            for rows in deep
            for _ in range(levels)
        ],
        scratch_shapes=[scratch],
        compiler_params=params(),
        name="spread",
    )(region_start, place, orbitals)
    across = pltpu.VMEM((count, cross), F32)
    home_sides, near_sides = [], []
    for which in range(chunks):
        mine = pieces[which * levels : (which + 1) * levels]
        got = [mine[0]] + [around(mine[by], by) for by in range(1, levels)]
        same = jnp.stack([item[0] for item in got])
        other = jnp.stack([item[1] for item in got])
        near_sides.append((onward(same), across_up(other)))
        home_sides.append((same, swapped(other)))

    def chunk_args(sides, which):
        arrays = list(sides[which])
        specs = whole(arrays)
        if which > 0:
            for side in range(2):
                for back_by in (2, 1):
                    item = sides[which - 1][side]
                    at = item.shape[1] - back_by
                    arrays.append(item)
                    specs.append(
                        pl.BlockSpec(
                            (levels, 1, held, cross), lambda t, at=at: (0, at, 0, 0)
                        )
                    )
        return arrays, specs

    fields = [
        shaped((cuts[i + 1] - cuts[i], count, 4 * cross)) for i in range(chunks)
    ]
    seat = shaped((count, 128), F32)
    homes, nears = [], []
    home_off = near_off = pair = table = None
    for which in range(chunks):
        arrays, specs = chunk_args(home_sides, which)
        fixed_args = [window_pot, kin_cross]
        outs = [fields[which]] * 2 + [shaped((2 * count, count), F32)]
        if which == 0:
            outs.append(seat)
            more = []
        else:
            more = [home_off, pair]
        result = call(
            functools.partial(own_kernel, which=which, cuts=cuts),
            outs,
            whole(fixed_args) + specs + whole(more),
            (place, *fixed_args, *arrays, *more),
            [across],
            1,
        )
        homes.append(result[:2])
        pair = result[2]
        if which == 0:
            home_off = result[3]
    packed = (2, 5 * 16, 2 * count)
    table_shape = (2, 2 * count + BLOCK, 2 * count)
    for which in range(chunks):
        arrays, specs = chunk_args(near_sides, which)
        fixed_args = [window_pot, kin_cross]
        last = which == chunks - 1
        more = list(homes[which])
        if last:
            more.append(pair)
        outs = [fields[which]] * 2
        if which == 0:
            outs.append(seat)
        else:
            more += [near_off, table]
        if last:
            outs += [shaped(packed, PARTIAL)] * 4
            temp = [pltpu.VMEM(table_shape, F32), across]
        else:
            outs += [shaped((2, 2 * count, 2 * count), F32)]
            temp = [across]
        result = call(
            functools.partial(near_kernel, which=which, cuts=cuts, scale=1.0 / (length * cross)),
            outs,
            whole(fixed_args) + specs + whole(more),
            (place, pattern, *fixed_args, *arrays, *more),
            temp,
            2,
        )
        nears.append(result[:2])
        rest = result[2:]
        if which == 0:
            near_off, rest = rest[0], rest[1:]
        if last:
            parts = rest
        else:
            table = rest[0]

    total = parts[0].astype(F32)
    for item in [around(parts[by], by) for by in range(1, levels)]:
        total = total + item.astype(F32)
    held_sum = total[:, :, :count] + back(total[:, :, count:].astype(PARTIAL)).astype(F32)
    done = (held_sum + swapped(held_sum)).astype(BF16)
    dones = jnp.stack([done] + [around(done, by) for by in range(1, levels)])
    passed = onward(dones)
    mat = call(
        unpack_kernel,
        shaped((2 * count, 4 * count)),
        whole([dones, passed]),
        (place, pattern, dones, passed),
        (),
        2,
    )
    got = []
    for which in range(chunks):
        wide = 4 * (cuts[which + 1] - cuts[which])
        more = [home_off, near_off, mat, *homes[which], *nears[which]]
        by_quad = pl.BlockSpec((1, count, 4 * cross), lambda t: (t, 0, 0))
        own_same, own_other, near_same, near_other = pl.pallas_call(
            functools.partial(
                gradient_kernel, start=cuts[which], scale=1.0 / (pattern.shape[1] * BLOCK)
            ),
            grid=(wide // 4,),
            out_shape=[shaped((levels, wide, held, cross))] * 4,
            in_specs=[smem()] + whole(more[:3]) + [by_quad] * 4,
            out_specs=[pl.BlockSpec((levels, 4, held, cross), lambda t: (0, t, 0, 0))] * 4,
            compiler_params=params(),
        )(place, *more)
        first, second = back(near_same), across_up(near_other)
        given = swapped(own_other)
        first = own_same + first
        second = given + second
        mine = [jnp.stack([first[d], second[d]]) for d in range(levels)]
        got += [mine[0]] + [around(mine[by], by) for by in range(1, levels)]
    return pl.pallas_call(
        functools.partial(collect_kernel, cuts=cuts),
        grid=(2,),
        out_shape=shaped(orbitals.shape),
        in_specs=[smem(), smem()]
        + [pl.BlockSpec((2, item.shape[1], part, cross), lambda t: (0, 0, t, 0)) for item in got],
        out_specs=by_part,
        scratch_shapes=[scratch],
        compiler_params=params(),
        name="collect",
    )(region_start, place, *got)


def solution(mesh):
    placed = (
        P(("slab", "orb"), None, None),
        P(("slab", "orb")),
        P(),
        P(("slab", "orb"), None),
        P(),
    )
    return jax.shard_map(
        body,
        mesh=mesh,
        in_specs=placed,
        out_specs=P(("slab", "orb"), None, None),
        check_vma=False,
    )
```

```python
import functools
import jax
import jax.numpy as jnp
from jax import lax
from jax.experimental import pallas as pl
from jax.experimental.pallas import tpu as pltpu
from jax.sharding import PartitionSpec as P

BLOCK = 64
CUTS = (0, 2, 4)
F32 = jnp.float32
BF16 = jnp.bfloat16
PARTIAL = BF16
NT = (((1,), (1,)), ((), ()))


def params():
    return pltpu.CompilerParams(vmem_limit_bytes=24 * 1024 * 1024)


def smem():
    return pl.BlockSpec(memory_space=pltpu.SMEM)


def vmem():
    return pl.BlockSpec(memory_space=pltpu.VMEM)


def near_core(array):
    return pltpu.with_memory_space_constraint(array, pltpu.VMEM)


def shaped(shape, dtype=BF16):
    return pltpu.VMEM(shape, dtype)


class Place:
    def __init__(self):
        slab = lax.axis_index("slab").astype(jnp.int32)
        orb = lax.axis_index("orb").astype(jnp.int32)
        slabs, levels = lax.axis_size("slab"), lax.axis_size("orb") // 2
        core, level = orb & 1, orb // 2
        near = lax.rem(slab + slabs - 1 + 2 * core, jnp.int32(slabs))
        position = (core * levels + level) * 16 + 64
        self.items = [position, slab, near, level, core]

    def __getitem__(self, at):
        return self.items[at]


def other_core(place_ref, side):
    return place_ref[4] if side == 0 else 1 - place_ref[4]


def spread_kernel(start_ref, x_ref, *rest, cuts):
    place_ref = Place()
    outs, scratch = rest[:-1], rest[-1]
    held, length, cross = x_ref.shape
    levels = 4
    narrow = length // (2 * levels)
    base = place_ref[1] * length
    gap = (
        lax.broadcasted_iota(jnp.int32, (length, length), 0)
        - lax.broadcasted_iota(jnp.int32, (length, length), 1)
    ) & (length - 1)
    mine = pl.ds(pl.multiple_of(pl.program_id(0) * held, held), held)
    which_row = lax.broadcasted_iota(jnp.int32, (held, cross), 0)
    offsets = jnp.zeros((held, cross), jnp.int32)
    for j in range(held):
        offset = start_ref[pl.program_id(0) * held + j] - base
        offsets = jnp.where(which_row == j, offset, offsets)
        shift = (offset + length // 2) & (length - 1)
        pick = jnp.where(gap == shift, 1.0, 0.0).astype(BF16)
        rolled = jnp.dot(pick, x_ref[j], preferred_element_type=F32)
        for half in range(cross // 128):
            scratch[half, pl.ds(j, length, stride=held), :] = rolled[:, half * 128 : half * 128 + 128]
    offsets = offsets.astype(F32).astype(BF16)
    for d in range(levels):
        for side in range(2):
            group = other_core(place_ref, side) * levels + ((place_ref[3] + d) & (levels - 1))
            outs[d][side, 0, mine, :] = offsets
            for which, (first, last) in enumerate(spans(cuts)):
                for q in range(first, last):
                    row = (group * narrow + q - 1) & (length - 1)
                    to = q - first + (1 if which == 0 else 0)
                    for half in range(cross // 128):
                        outs[which * levels + d][side, to, mine, half * 128 : half * 128 + 128] = scratch[
                            half, pl.ds(pl.multiple_of(row * held, held), held), :
                        ].astype(BF16)


def spans(cuts):
    return [
        (0 if i == 0 else 4 * cuts[i] + 2, 4 * cuts[i + 1] + 2) for i in range(len(cuts) - 1)
    ]


def collect_kernel(start_ref, *rest, cuts):
    place_ref = Place()
    levels = 4
    out_ref, scratch = rest[-2], rest[-1]
    held, length, cross = out_ref.shape
    narrow = length // (2 * levels)
    base = place_ref[1] * length + length // 2
    gap = (
        lax.broadcasted_iota(jnp.int32, (length, length), 1)
        - lax.broadcasted_iota(jnp.int32, (length, length), 0)
    ) & (length - 1)
    mine = pl.ds(pl.multiple_of(pl.program_id(0) * held, held), held)
    for which in range(len(cuts) - 1):
        wide = 4 * (cuts[which + 1] - cuts[which])
        for d in range(levels):
            for side in range(2):
                group = other_core(place_ref, side) * levels + ((place_ref[3] - d) & (levels - 1))
                first = (group * narrow + 4 * cuts[which]) * held
                for half in range(cross // 128):
                    scratch[half, pl.ds(pl.multiple_of(first, 4 * held), wide * held), :] = (
                        rest[which * levels + d][side, :, mine, half * 128 : half * 128 + 128]
                        .reshape(wide * held, 128)
                        .astype(F32)
                    )
    for j in range(held):
        shift = (start_ref[pl.program_id(0) * held + j] - base) & (length - 1)
        pick = jnp.where(gap == shift, 1.0, 0.0).astype(BF16)
        rows = jnp.concatenate(
            [scratch[half, pl.ds(j, length, stride=held), :] for half in range(cross // 128)], axis=1
        ).astype(BF16)
        out_ref[j] = jnp.dot(pick, rows, preferred_element_type=F32).astype(BF16)


def make_fields(place_ref, pot_ref, kin_ref, off_ref, row_at, across_ref, phi_ref, app_ref, *, own, start):
    cross = kin_ref.shape[0]
    quads, count, _ = phi_ref.shape
    levels = 4
    held = count // (2 * levels)
    units = [(d, side) for d in range(levels) for side in range(2)]
    places = [
        pl.multiple_of(
            (((place_ref[3] - d) & (levels - 1)) * 2 + other_core(place_ref, side)) * held, held
        )
        for d, side in units
    ]
    for col in range(4 * quads):
        lanes = slice((col % 4) * cross, (col % 4 + 1) * cross)
        now = start * 4 + col
        for (d, side), at in zip(units, places):
            place = place_ref[0] + now - off_ref[pl.ds(at, held), :]
            inside = (place & -128) == 0
            keep = jnp.where(inside, 1.0, 0.0) if own else jnp.where(inside, 0.0, 1.0)
            keep = keep.astype(BF16)
            keep = jnp.concatenate([keep, keep], axis=1)
            phi_ref[col // 4, pl.ds(at, held), lanes] = row_at(side, d, now + 1) * keep
        across_ref[...] = jnp.dot(
            phi_ref[col // 4, :, lanes], kin_ref[...], preferred_element_type=F32
        )
        for (d, side), at in zip(units, places):
            place = place_ref[0] + now - off_ref[pl.ds(at, held), :]
            inside = (place & -128) == 0
            keep = jnp.where(inside, 0.5, 0.0) if own else jnp.where(inside, 0.0, 0.5)
            row = place & 127
            left = jnp.where(row == 0, 0.0, keep).astype(BF16)
            right = jnp.where(row == 127, 0.0, keep).astype(BF16)
            left = jnp.concatenate([left, left], axis=1)
            right = jnp.concatenate([right, right], axis=1)
            phi = phi_ref[col // 4, pl.ds(at, held), lanes].astype(F32)
            around = (row_at(side, d, now) * left).astype(F32) + (
                row_at(side, d, now + 2) * right
            ).astype(F32)
            kin = (phi - around + across_ref[pl.ds(at, held), :]).astype(BF16).astype(F32)
            app_ref[col // 4, pl.ds(at, held), lanes] = (
                kin + pot_ref[now : now + 1, :] * phi
            ).astype(BF16)


def chunk_inputs(refs, which, cuts):
    if which == 0:
        pair, rest = refs[:2], refs[2:]

        def row_at(side, d, q):
            return pair[side][d, q + 1]

        return row_at, rest
    pair, edges, rest = refs[:2], refs[2:4], refs[4:]
    first = spans(cuts)[which][0]

    def row_at(side, d, q):
        if q >= first:
            return pair[side][d, q - first]
        return edges[side][d, edges[side].shape[1] + q - first]

    return row_at, rest


def own_kernel(pot_ref, kin_ref, *refs, which, cuts):
    place_ref = Place()
    row_at, rest = chunk_inputs(refs, which, cuts)
    if which == 0:
        phi_ref, app_ref, pair_ref, off_ref, across_ref = rest
        store_offsets(place_ref, refs, off_ref)
    else:
        off_ref, before_ref, phi_ref, app_ref, pair_ref, across_ref = rest
    make_fields(
        place_ref, pot_ref, kin_ref, off_ref, row_at, across_ref, phi_ref, app_ref,
        own=True, start=cuts[which],
    )
    for quad in range(phi_ref.shape[0]):
        phi = phi_ref[quad]
        both = jnp.concatenate([phi, app_ref[quad]], axis=0)
        term = lax.dot_general(both, phi, NT, preferred_element_type=F32)
        if quad > 0:
            pair_ref[...] += term
        elif which == 0:
            pair_ref[...] = term
        else:
            pair_ref[...] = before_ref[...] + term


def store_offsets(place_ref, refs, off_ref):
    levels, _, held, _ = refs[0].shape
    for side in range(2):
        for d in range(levels):
            unit = ((place_ref[3] - d) & (levels - 1)) * 2 + other_core(place_ref, side)
            off_ref[pl.ds(pl.multiple_of(unit * held, held), held), :] = (
                refs[side][d, 0][:, :128].astype(F32).astype(jnp.int32)
            )


def near_kernel(pattern_ref, pot_ref, kin_ref, *refs, which, cuts, scale):
    place_ref = Place()
    row_at, rest = chunk_inputs(refs, which, cuts)
    last = which == len(cuts) - 2
    phi_own_ref, app_own_ref, rest = rest[0], rest[1], rest[2:]
    if last:
        pair_ref, rest = rest[0], rest[1:]
    if which == 0:
        phi_ref, app_ref, off_ref, rest = rest[0], rest[1], rest[2], rest[3:]
        store_offsets(place_ref, refs, off_ref)
    else:
        off_ref, before_ref, phi_ref, app_ref, rest = rest[0], rest[1], rest[2], rest[3], rest[4:]
    if last:
        outs, table, across_ref = rest[:4], rest[4], rest[5]
    else:
        table, across_ref = rest
    make_fields(
        place_ref, pot_ref, kin_ref, off_ref, row_at, across_ref, phi_ref, app_ref,
        own=False, start=cuts[which],
    )
    count = phi_ref.shape[1]
    for quad in range(phi_ref.shape[0]):
        phi_own, app_own, phi, app = phi_own_ref[quad], app_own_ref[quad], phi_ref[quad], app_ref[quad]
        every = jnp.concatenate([phi_own, phi, app_own, app], axis=0)
        near = lax.dot_general(every, phi, NT, preferred_element_type=F32)
        both = jnp.concatenate([phi, app], axis=0)
        home = lax.dot_general(both, phi_own, NT, preferred_element_type=F32)
        for kind in range(2):
            right = near[kind * 2 * count : (kind + 1) * 2 * count]
            left = home[kind * count : (kind + 1) * count]
            if quad > 0:
                table[kind, : 2 * count, count:] += right
                table[kind, count : 2 * count, :count] += left
            elif which > 0:
                table[kind, : 2 * count, count:] = right + before_ref[kind, : 2 * count, count:]
                table[kind, count : 2 * count, :count] = (
                    left + before_ref[kind, count : 2 * count, :count]
                )
            else:
                table[kind, : 2 * count, count:] = right
                table[kind, count : 2 * count, :count] = left
    if not last:
        return
    for kind in range(2):
        table[kind, :count, :count] = pair_ref[kind * count : (kind + 1) * count]
        table[kind, 2 * count :, :] = jnp.zeros_like(table[kind, 2 * count :, :])
    low = lax.broadcasted_iota(jnp.int32, (16, 128), 1) < BLOCK
    per_slab = count // BLOCK
    for group in range(2 * count // 128):
        for slot in range(5):
            first, second = [
                local_block(place_ref, pattern_ref, 2 * group + side, slot, per_slab) * BLOCK
                for side in range(2)
            ]
            for by in range(4):
                quarter = ((place_ref[3] + by) & 3) * 16
                for kind in range(2):
                    lanes = slice(group * 128, group * 128 + 128)
                    one = table[kind, pl.ds(pl.multiple_of(first + quarter, 16), 16), lanes]
                    two = table[kind, pl.ds(pl.multiple_of(second + quarter, 16), 16), lanes]
                    outs[by][kind, slot * 16 : slot * 16 + 16, lanes] = (
                        jnp.where(low, one, two) * scale
                    ).astype(outs[by].dtype)


def local_block(place_ref, pattern_ref, block, slot, per_slab):
    home, near = place_ref[1], place_ref[2]
    base = home if block < per_slab else near
    listed = pattern_ref[slot, base * per_slab + block % per_slab]
    slab = listed // per_slab
    inner = listed % per_slab
    return jnp.where(slab == home, inner, jnp.where(slab == near, per_slab + inner, 2 * per_slab))


def unpack_kernel(pattern_ref, *rest):
    place_ref = Place()
    out_ref = rest[8]
    total = out_ref.shape[0]
    per_slab = total // 2 // BLOCK
    low = lax.broadcasted_iota(jnp.int32, (16, 128), 1) < BLOCK
    for group in range(total // 128):
        parts = rest[:4] if group < total // 256 else rest[4:8]
        first = group * 128 % (total // 2)
        lanes = slice(first, first + 128)
        found = []
        for slot in range(5):
            first, second = [
                local_block(place_ref, pattern_ref, 2 * group + side, slot, per_slab)
                for side in range(2)
            ]
            found.append(jnp.where(low, first, second))
        for block in range(2 * per_slab):
            hits = [
                jnp.where(found[slot] == block, 1.0, 0.0).astype(BF16) for slot in range(5)
            ]
            for by in range(4):
                quarter = (place_ref[3] - by) & 3
                side = (quarter // 2) ^ place_ref[4]
                d = (block % per_slab - place_ref[3]) & 3
                row = ((block // per_slab * 2 + side) * 4 + d) * 32 + (quarter % 2) * 16
                for kind in range(2):
                    terms = [
                        parts[by][kind, slot * 16 : slot * 16 + 16, lanes] * hits[slot]
                        for slot in range(5)
                    ]
                    acc = (terms[0] + terms[1]) + (terms[2] + terms[3]) + terms[4]
                    if kind == 1:
                        acc = -acc
                    out_ref[
                        pl.ds(pl.multiple_of(row, 16), 16),
                        kind * total + group * 128 : kind * total + group * 128 + 128,
                    ] = acc


def gradient_kernel(off_own_ref, off_near_ref, mat_ref, *rest, start, scale):
    place_ref = Place()
    ins, outs = rest[:4], rest[4:]
    levels, _, held, cross = outs[0].shape
    phi_own_ref, app_own_ref, phi_ref, app_ref = ins
    seats = []
    for ref in (off_own_ref, off_near_ref):
        for side in range(2):
            for d in range(levels):
                unit = ((place_ref[3] + d) & (levels - 1)) * 2 + other_core(place_ref, side)
                seats.append(
                    ref[pl.ds(pl.multiple_of(unit * held, held), held), :]
                )
    quad = pl.program_id(0)
    right = jnp.concatenate(
        [app_own_ref[quad], app_ref[quad], phi_own_ref[quad], phi_ref[quad]], axis=0
    )
    grad = jnp.dot(mat_ref[...], right, preferred_element_type=F32)
    base = place_ref[0] + start * 4 + quad * 4
    for step in range(4):
        for i, seat in enumerate(seats):
            inside = ((base + step - seat) & -128) == 0
            own = i < 2 * levels
            keep = jnp.where(inside, scale, 0.0) if own else jnp.where(inside, 0.0, scale)
            keep = jnp.concatenate([keep, keep], axis=1)
            part = grad[i * held : (i + 1) * held, step * cross : (step + 1) * cross] * keep
            outs[i // levels][i % levels, quad * 4 + step] = part.astype(BF16)


def body(orbitals, region_start, kin_cross, potential, pattern):
    held, length, cross = orbitals.shape
    peers = lax.axis_size("orb")
    slabs = lax.axis_size("slab")
    levels = peers // 2
    count = held * peers
    narrow = length // peers
    axes = ("slab", "orb")
    cuts = CUTS
    chunks = len(cuts) - 1

    def send(array, route):
        pairs = []
        for s in range(slabs):
            for k in range(peers):
                ds, dk = route(k % 2, k // 2)
                pairs.append((s * peers + k, ((s + ds) % slabs) * peers + dk))
        return lax.ppermute(array, axes, pairs)

    def onward(array):
        return send(array, lambda c, y: ((1, 2 * y) if c == 0 else (-1, 2 * y + 1)))

    def back(array):
        return send(array, lambda c, y: ((-1, 2 * y) if c == 0 else (1, 2 * y + 1)))

    def across_up(array):
        return send(array, lambda c, y: ((-1, 2 * y + 1) if c == 0 else (1, 2 * y)))

    def swapped(array):
        return send(array, lambda c, y: (0, 2 * y + 1 - c))

    def around(array, by):
        return send(array, lambda c, y: (0, 2 * ((y + by) % levels) + c))

    pot_pairs = []
    for s in range(slabs):
        for k in range(peers):
            if k >= levels:
                pot_pairs.append((s * peers + k, s * peers + 2 * (k - levels)))
            else:
                pot_pairs.append((s * peers + k, ((s - 1) % slabs) * peers + 2 * k + 1))
    window_pot = lax.ppermute(potential, axes, pot_pairs)

    def call(kernel, outs, args, scratch=(), smems=0, grid=(1,), slow=()):
        def spec(item, far):
            return pl.BlockSpec(item.shape, lambda t: (0,) * len(item.shape)) if far else vmem()

        first, arrays = args[:smems], args[smems:]
        far = [any(item is other for other in slow) for item in arrays]
        return pl.pallas_call(
            kernel,
            grid=grid,
            out_shape=outs,
            in_specs=[smem()] * smems + [spec(*pair) for pair in zip(arrays, far)],
            out_specs=[spec(item, isinstance(item, jax.ShapeDtypeStruct)) for item in outs],
            scratch_shapes=list(scratch),
            compiler_params=params(),
        )(*first, *[item if away else near_core(item) for item, away in zip(arrays, far)])

    def far_off(array):
        return pltpu.with_memory_space_constraint(array, pltpu.HBM)

    orbitals, region_start = far_off(orbitals), far_off(region_start)
    part = held // 2
    scratch = pltpu.VMEM((cross // 128, length * part, 128), F32)
    deep = [last - first + (1 if i == 0 else 0) for i, (first, last) in enumerate(spans(cuts))]
    by_part = pl.BlockSpec((part, length, cross), lambda t: (t, 0, 0))
    pieces = pl.pallas_call(
        functools.partial(spread_kernel, cuts=cuts),
        grid=(2,),
        out_shape=[shaped((2, rows, held, cross)) for rows in deep for _ in range(levels)],
        in_specs=[smem(), by_part],
        out_specs=[vmem()] * (len(deep) * levels),
        scratch_shapes=[scratch],
        compiler_params=params(),
        name="spread",
    )(region_start, orbitals)
    across = pltpu.VMEM((count, cross), F32)
    home_sides, near_sides = [], []
    for which in range(chunks):
        mine = pieces[which * levels : (which + 1) * levels]
        got = [mine[0]] + [around(mine[by], by) for by in range(1, levels)]
        same = jnp.stack([item[0] for item in got])
        other = jnp.stack([item[1] for item in got])
        near_sides.append((onward(same), across_up(other)))
        home_sides.append((same, swapped(other)))

    def chunk_args(sides, which):
        return list(sides[which]) + (list(sides[which - 1]) if which > 0 else [])

    fields = [
        shaped((cuts[i + 1] - cuts[i], count, 4 * cross)) for i in range(chunks)
    ]
    seat = jax.ShapeDtypeStruct((count, 128), jnp.int32)
    homes, nears = [], []
    home_off = near_off = pair = table = None
    for which in range(chunks):
        arrays = chunk_args(home_sides, which)
        fixed_args = [window_pot, kin_cross]
        outs = [fields[which]] * 2 + [jax.ShapeDtypeStruct((2 * count, count), F32)]
        if which == 0:
            outs.append(seat)
            more = []
        else:
            more = [home_off, pair]
        result = call(
            functools.partial(own_kernel, which=which, cuts=cuts),
            outs,
            [*fixed_args, *arrays, *more],
            [across],
            slow=[home_off, pair],
        )
        homes.append(result[:2])
        pair = result[2]
        if which == 0:
            home_off = result[3]
    packed = (2, 5 * 16, 2 * count)
    table_shape = (2, 2 * count + BLOCK, 2 * count)
    for which in range(chunks):
        arrays = chunk_args(near_sides, which)
        fixed_args = [window_pot, kin_cross]
        last = which == chunks - 1
        more = list(homes[which])
        if last:
            more.append(pair)
        outs = [fields[which]] * 2
        if which == 0:
            outs.append(seat)
        else:
            more += [near_off, table]
        if last:
            outs += [shaped(packed, PARTIAL)] * 4
            temp = [pltpu.VMEM(table_shape, F32), across]
        else:
            outs += [shaped((2, 2 * count, 2 * count), F32)]
            temp = [across]
        result = call(
            functools.partial(near_kernel, which=which, cuts=cuts, scale=1.0 / (length * cross)),
            outs,
            (pattern.T, *fixed_args, *arrays, *more),
            temp,
            1,
            slow=[near_off, pair],
        )
        nears.append(result[:2])
        rest = result[2:]
        if which == 0:
            near_off, rest = rest[0], rest[1:]
        if last:
            parts = rest
        else:
            table = rest[0]

    total = parts[0].astype(F32)
    for item in [around(parts[by], by) for by in range(1, levels)]:
        total = total + item.astype(F32)
    held_sum = total[:, :, :count] + back(total[:, :, count:].astype(PARTIAL)).astype(F32)
    done = (held_sum + swapped(held_sum)).astype(BF16)
    dones = [done] + [around(done, by) for by in range(1, levels)]
    passed = [
        send(
            done,
            lambda c, y, by=by: (
                (1, 2 * ((y + by) % levels)) if c == 0 else (-1, 2 * ((y + by) % levels) + 1)
            ),
        )
        for by in range(levels)
    ]
    mat = call(
        unpack_kernel, [shaped((2 * count, 4 * count))], (pattern.T, *dones, *passed), (), 1
    )[0]
    got = []
    for which in range(chunks):
        wide = 4 * (cuts[which + 1] - cuts[which])
        more = [home_off, near_off, mat, *homes[which], *nears[which]]
        own_same, own_other, near_same, near_other = call(
            functools.partial(
                gradient_kernel, start=cuts[which], scale=1.0 / (pattern.shape[1] * BLOCK)
            ),
            [shaped((levels, wide, held, cross))] * 4,
            [*more],
            (),
            0,
            (wide // 4,),
            [home_off, near_off],
        )
        first, second = back(near_same), across_up(near_other)
        given = swapped(own_other)
        first = own_same + first
        second = given + second
        mine = [jnp.stack([first[d], second[d]]) for d in range(levels)]
        got += [mine[0]] + [around(mine[by], by) for by in range(1, levels)]
    return pl.pallas_call(
        functools.partial(collect_kernel, cuts=cuts),
        grid=(2,),
        out_shape=jax.ShapeDtypeStruct(orbitals.shape, BF16),
        in_specs=[smem()] + [vmem()] * len(got),
        out_specs=by_part,
        scratch_shapes=[scratch],
        compiler_params=params(),
        name="collect",
    )(region_start, *map(near_core, got))


def solution(mesh):
    placed = (
        P(("slab", "orb"), None, None),
        P(("slab", "orb")),
        P(),
        P(("slab", "orb"), None),
        P(),
    )
    return jax.shard_map(
        body,
        mesh=mesh,
        in_specs=placed,
        out_specs=P(("slab", "orb"), None, None),
        check_vma=False,
    )
```
